256 devices in a mesh: seq: 32 (over y_lo, z, core), tensor: 8 (over y_hi, x).
Axes of the slice: x: 4, y: 4 (y_hi: 2, y_lo: 2; y = y_hi * 2 + y_lo), z: 8, core: 2. Of those that a mesh axis runs over, the one named last changes fastest.
Arguments:
- features: bfloat16 [4096, 3072], P('seq', 'tensor'), may hold values from -6 to 6
- gain: float32 [3072], replicated, may hold values from 0.1 to 1.9
- w_qkv: bfloat16 [3072, 3, 3072], P(None, None, 'tensor'), may hold values from -0.109375 to 0.109375
- rope_factors: float32 [48], replicated, may hold values from 1 to 64
- cache_len: int32 [4], replicated, may hold values from 1 to 12288, as said below
- cache_kv: bfloat16 [384, 128, 2, 3072], P('seq', None, None, 'tensor'), may hold values from -405 to 405, as said below
- block_owner: int32 [384], P('seq'), may hold values from 0 to 4, as said below
- block_base: int32 [384], P('seq'), may hold values from 0 to 12160, as said below
Outputs:
- attended: bfloat16 [4096, 3072], P('seq', 'tensor')
- new_kv: bfloat16 [4096, 2, 3072], P('seq', None, 'tensor')
The draws below stay inside these ranges and needn't reach their ends.
Inputs may be any that keep to these rules, and one draw needn't show every extreme that they name: `cache_len`: one request has exactly 12288 cached tokens; the others have between 1 and 9216. `block_owner`: request r owns exactly ceil(cache_len[r] / 128) blocks, placed anywhere in the pool; 4 marks a free block, and some blocks are free. `block_base`: the blocks of request r carry the bases 0, 128, 256, ... below cache_len[r], each once; free blocks carry 0. `cache_kv`: stored keys are already rotated.
All inputs are finite; a program needn't handle non-finite values.
Results may differ from the reference program's by a relative error of at most 0.014.
The reference program's roundings to bfloat16 on the way (of `normed`) count: a program that leaves them out, or rounds other values in their place, can miss the bound.
Values may be sent and summed in bfloat16 or wider, within the bound.
No kernel may reach another device: no remote copies, remote signals or barrier semaphores. Data moves between devices by JAX's collectives and lax.ppermute only.
A program may use at most 384 MiB of HBM per device.

```python
import math
import jax
import jax.numpy as jnp
from jax import lax

D = 3072
HEADS = 32
HD = 96
REQ = 4
BLK = 128
TOKENS = 4096
NEW = 1024
NBLK = 384
CACHE_MAX = 12288
OTHER = 9216


def cache_layout(key):
    base_key = jax.random.fold_in(key, 11)
    pick_key, shift_key, size_key, shuffle_key = jax.random.split(base_key, 4)
    longest = jax.random.randint(pick_key, (), 0, REQ)
    shifts = jax.random.randint(shift_key, (REQ,), 0, 4)
    ceilings = jnp.right_shift(jnp.full((REQ,), OTHER, jnp.int32), shifts.astype(jnp.int32))
    others = jax.random.randint(size_key, (REQ,), 1, ceilings + 1)
    lengths = jnp.where(jnp.arange(REQ) == longest, CACHE_MAX, others).astype(jnp.int32)
    counts = (lengths + BLK - 1) // BLK
    closing = jnp.cumsum(counts)
    opening = closing - counts
    slot_ids = jnp.arange(NBLK, dtype=jnp.int32)
    owners = jnp.sum((slot_ids[:, None] >= closing[None, :]).astype(jnp.int32), axis=1).astype(jnp.int32)
    clamped = jnp.minimum(owners, REQ - 1)
    offsets = jnp.where(owners < REQ, (slot_ids - opening[clamped]) * BLK, 0).astype(jnp.int32)
    shuffle = jax.random.permutation(shuffle_key, NBLK)
    owner_array = jnp.zeros((NBLK,), jnp.int32).at[shuffle].set(owners)
    base_array = jnp.zeros((NBLK,), jnp.int32).at[shuffle].set(offsets)
    return (lengths, owner_array, base_array)


def draw_cache_len(key, part):
    return cache_layout(key)[0]


def draw_block_owner(key, part):
    return cache_layout(key)[1]


def draw_block_base(key, part):
    return cache_layout(key)[2]


def draw_cache_kv(key, part):
    value_key = jax.random.fold_in(jax.random.fold_in(key, 23), 0)
    entries = jnp.clip(jax.random.normal(value_key, (NBLK, BLK, 2, HEADS * HD), jnp.float32), -5.0, 5.0)
    return entries.astype(jnp.bfloat16)


def steps_of(rng, dims, shards, low, largest):
    level = 1.0
    for axis_at, shards_of in shards:
        steps = jax.random.uniform(jax.random.fold_in(jax.random.fold_in(rng, 6), axis_at), (shards_of,), jnp.float32, low / len(shards), largest / len(shards))
        level = level * jnp.repeat(jnp.exp(steps), dims[axis_at] // shards_of).reshape((-1,) + (1,) * (len(dims) - 1 - axis_at))
    return level


def scatter_about(rng, shape, deviation, limit, shards=(), held_as=jnp.bfloat16):
    values = deviation * jax.random.normal(rng, shape, jnp.float32)
    if shards:
        values = values * steps_of(rng, shape, shards, -0.22, 0.18)
    return jnp.clip(values, -limit, limit).astype(held_as)


def setup_inputs(seed: int = 0) -> dict:
    key_of = jax.random.split(jax.random.key(seed), 9)
    features = scatter_about(key_of[0], (TOKENS, D), 1.0, 6.0, ((0, 32), (1, 8)))
    gain = jnp.clip(1.0 + 0.18 * jax.random.normal(key_of[1], (D,), jnp.float32), 0.1, 1.9)
    w_qkv = scatter_about(key_of[2], (D, 3, HEADS * HD), D ** -0.5, 0.109375, ((2, 8),))
    rope_factors = jnp.clip(jnp.exp(jax.random.uniform(key_of[3], (HD // 2,), jnp.float32, math.log(1.0), math.log(64.0))), 1.0, 64.0)
    cache_len = draw_cache_len(jax.random.fold_in(key_of[8], 71), 0)
    cache_kv = draw_cache_kv(jax.random.fold_in(key_of[8], 71), 0)
    block_owner = draw_block_owner(jax.random.fold_in(key_of[8], 71), 0)
    block_base = draw_block_base(jax.random.fold_in(key_of[8], 71), 0)
    return dict(features=features, gain=gain, w_qkv=w_qkv, rope_factors=rope_factors, cache_len=cache_len, cache_kv=cache_kv, block_owner=block_owner, block_base=block_base)


EPSILON = 1e-05
NEGATIVE = -1e+30
MSCALE = 1.1902380714238083

def rotate(vectors, angles):
    half_dim = vectors.shape[-1] // 2
    front_half = vectors[..., :half_dim]
    back_half = vectors[..., half_dim:]
    cosine = jnp.cos(angles) * MSCALE
    sine_part = jnp.sin(angles) * MSCALE
    return jnp.concatenate([front_half * cosine - back_half * sine_part, back_half * cosine + front_half * sine_part], axis=-1)

def pick_row(array, where_at):
    return lax.dynamic_index_in_dim(array, where_at, 0, keepdims=False)

def put_row(array, update, where_at):
    return lax.dynamic_update_index_in_dim(array, update, where_at, 0)

def reference(features, gain, w_qkv, rope_factors, cache_len, cache_kv, block_owner, block_base):
    wide_x = features.astype(jnp.float32)
    normed = (wide_x * lax.rsqrt(lax.optimization_barrier(jnp.mean(wide_x * wide_x, axis=1, keepdims=True)) + EPSILON) * gain).astype(jnp.bfloat16)
    projected = jnp.einsum('td,dcf->tcf', normed.astype(jnp.float32), w_qkv.astype(jnp.float32))
    row_ids = jnp.arange(TOKENS, dtype=jnp.int32)
    positions = cache_len[row_ids // NEW] + row_ids % NEW
    inv_freq = 1.0 / (rope_factors * jnp.power(10000.0, jnp.arange(HD // 2, dtype=jnp.float32) * 2.0 / HD))
    angles = positions.astype(jnp.float32)[:, None, None] * inv_freq[None, None, :]
    shaped = projected.reshape(TOKENS, 3, HEADS, HD)
    queries = (rotate(shaped[:, 0], angles) * HD ** (-0.5)).astype(jnp.bfloat16)
    new_keys = rotate(shaped[:, 1], angles).astype(jnp.bfloat16)
    new_values = shaped[:, 2].astype(jnp.bfloat16)
    new_kv = jnp.stack([new_keys.reshape(TOKENS, HEADS * HD), new_values.reshape(TOKENS, HEADS * HD)], axis=1)
    query_req = queries.reshape(REQ, NEW, HEADS, HD)
    key_req = new_keys.reshape(REQ, NEW, HEADS, HD)
    value_req = new_values.reshape(REQ, NEW, HEADS, HD)
    own_pos = positions.reshape(REQ, NEW)
    causal = own_pos[:, None, :] <= own_pos[:, :, None]
    cache_keys = cache_kv[:, :, 0].reshape(NBLK, BLK, HEADS, HD)
    cache_values = cache_kv[:, :, 1].reshape(NBLK, BLK, HEADS, HD)
    clamped = jnp.minimum(block_owner, REQ - 1)
    bound_len = jnp.where(block_owner < REQ, cache_len[clamped], 0)
    usable = block_base[:, None] + jnp.arange(BLK, dtype=jnp.int32)[None, :] < bound_len[:, None]

    def one_head(head_id):
        head_q = lax.dynamic_index_in_dim(query_req, head_id, 2, keepdims=False)
        head_k = lax.dynamic_index_in_dim(key_req, head_id, 2, keepdims=False)
        head_v = lax.dynamic_index_in_dim(value_req, head_id, 2, keepdims=False)
        block_k = lax.dynamic_index_in_dim(cache_keys, head_id, 2, keepdims=False)
        block_v = lax.dynamic_index_in_dim(cache_values, head_id, 2, keepdims=False)
        new_scores = jnp.einsum('rnd,rkd->rnk', head_q.astype(jnp.float32), head_k.astype(jnp.float32))
        maxima = lax.optimization_barrier(jnp.max(jnp.where(causal, new_scores, NEGATIVE), axis=2))

        def first_step(running, paired):
            keys_b, usable_b, owner_b = paired
            scores = jnp.dot(pick_row(head_q, owner_b), keys_b.T, preferred_element_type=jnp.float32)
            block_max = lax.optimization_barrier(jnp.max(jnp.where(usable_b[None, :], scores, NEGATIVE), axis=1))
            return (put_row(running, jnp.maximum(pick_row(running, owner_b), block_max), owner_b), None)
        maxima = lax.scan(first_step, maxima, (block_k, usable, clamped))[0]
        weight = jnp.where(causal, jnp.exp(new_scores - maxima[:, :, None]), 0.0)
        rounded = lax.optimization_barrier(weight.astype(jnp.bfloat16))
        numerator = jnp.einsum('rnk,rkd->rnd', rounded.astype(jnp.float32), head_v.astype(jnp.float32))
        denominator = lax.optimization_barrier(jnp.sum(weight, axis=2))

        def second_step(running, paired):
            keys_b, values_b, usable_b, owner_b = paired
            numer_now, denom_now = running
            scores = jnp.dot(pick_row(head_q, owner_b), keys_b.T, preferred_element_type=jnp.float32)
            block_weight = jnp.where(usable_b[None, :], jnp.exp(scores - pick_row(maxima, owner_b)[:, None]), 0.0)
            term = jnp.dot(block_weight.astype(jnp.bfloat16), values_b, preferred_element_type=jnp.float32)
            numer_now = put_row(numer_now, pick_row(numer_now, owner_b) + term, owner_b)
            denom_now = put_row(denom_now, pick_row(denom_now, owner_b) + lax.optimization_barrier(jnp.sum(block_weight, axis=1)), owner_b)
            return ((numer_now, denom_now), None)
        numerator, denominator = lax.scan(second_step, (numerator, denominator), (block_k, block_v, usable, clamped))[0]
        return (numerator / denominator[:, :, None]).astype(jnp.bfloat16)
    per_head = lax.map(one_head, jnp.arange(HEADS, dtype=jnp.int32))
    attended = per_head.transpose(1, 2, 0, 3).reshape(TOKENS, HEADS * HD)
    return (attended, new_kv)
```

```python
import functools

import jax
import jax.numpy as jnp
from jax import lax
from jax.experimental import pallas as pl
from jax.experimental.pallas import tpu as pltpu
from jax.sharding import Mesh, PartitionSpec as P


S = jax.ShapeDtypeStruct
EPSILON = 1e-05
NEG = -1e30
FLOOR = -1e29
MSCALE = 1.1902380714238083
F32 = jnp.float32
BF = jnp.bfloat16
I32 = jnp.int32
VM = pl.BlockSpec(memory_space=pltpu.VMEM)
SM = pl.BlockSpec(memory_space=pltpu.SMEM)
HBM = pl.BlockSpec(memory_space=pl.ANY)
HD = 96
HALF = 6
WIN = ((0,), (0, 1), (1, 2), (2,))
DIST = (4, 3, 5, 2, 6, 1, 7)


def ring(n, k):
    return [(i, (i + k) % n) for i in range(n)]


def pick(first):
    i = lax.broadcasted_iota(I32, (128, 256), 0)
    j = lax.broadcasted_iota(I32, (128, 256), 1)
    return (j == 2 * i + first).astype(F32).astype(BF)


def prep_body(kv_ref, o_ref):
    x = kv_ref[...].reshape(256, 384)
    k = jnp.dot(pick(0), x, preferred_element_type=F32).astype(BF)
    v = jnp.dot(pick(1), x, preferred_element_type=F32)
    for t in range(3):
        o_ref[128 * t:128 * t + 128] = k[:, 128 * t:128 * t + 128]
    o_ref[384:768] = v.T.astype(BF)


def prep(kv, first):
    return pl.pallas_call(
        prep_body,
        grid=(HALF,),
        in_specs=[pl.BlockSpec((None, 128, 2, 384), lambda i: (i + first, 0, 0, 0))],
        out_specs=pl.BlockSpec((None, 768, 128), lambda i: (i, 0, 0)),
        out_shape=S((HALF, 768, 128), BF),
        name="prep",
    )(kv)


def rotate(t, cos, sin):
    out = []
    for h in range(4):
        a = t[HD * h:HD * h + 48]
        b = t[HD * h + 48:HD * h + 96]
        out.append(a * cos - b * sin)
        out.append(b * cos + a * sin)
    return jnp.concatenate(out, axis=0)


def chunk_ids():
    yh = lax.axis_index("yh")
    x = lax.axis_index("x")
    ids = []
    for dx in (0, 3, 1, 2):
        xs = lax.rem(x + dx, 4)
        ids += [yh * 4 + xs, (1 - yh) * 4 + xs]
    return ids


def query_body(gain_ref, cos_ref, sin_ref, f0, f1, fr, fl, fm, w_hbm, q_ref, n_ref, wbuf, sem):
    ids = chunk_ids()
    copies = []
    for j in range(8):
        rows = pl.ds(pl.multiple_of(ids[j] * 384, 384), 384)
        c = pltpu.make_async_copy(w_hbm.at[0, rows], wbuf.at[j], sem.at[j])
        c.start()
        copies.append(c)
    chunks = [f0[...], f1[...]]
    for f in (fr, fl, fm):
        chunks += [f[0:128], f[128:256]]
    wide = [c.astype(F32) for c in chunks]
    total = jnp.zeros((128, 384), F32)
    for x in wide:
        total = total + x * x
    scale = lax.rsqrt(jnp.sum(total, axis=1, keepdims=True) * (1.0 / 3072) + EPSILON)
    acc = jnp.zeros((128, 384), F32)
    for j in range(8):
        n = (wide[j] * scale * gain_ref[ids[j]]).astype(BF)
        n_ref[j] = n
        copies[j].wait()
        acc = acc + jnp.dot(n, wbuf[j], preferred_element_type=F32)
    q_ref[...] = (rotate(acc.T, cos_ref[...], sin_ref[...]) * HD ** (-0.5)).astype(BF)


def keyval_body(cos_ref, sin_ref, n_ref, w_hbm, new_ref, k_ref, v_ref, wbuf, sem):
    ids = chunk_ids()
    copies = []
    for c in range(2):
        for j in range(8):
            rows = pl.ds(pl.multiple_of(ids[j] * 384, 384), 384)
            d = pltpu.make_async_copy(w_hbm.at[1 + c, rows], wbuf.at[c, j], sem.at[c, j])
            d.start()
            copies.append(d)
    accs = []
    for c in range(2):
        acc = jnp.zeros((128, 384), F32)
        for j in range(8):
            copies[8 * c + j].wait()
            acc = acc + jnp.dot(n_ref[j], wbuf[c, j], preferred_element_type=F32)
        accs.append(acc)
    k = rotate(accs[0].T, cos_ref[...], sin_ref[...]).T.astype(BF)
    v = accs[1]
    k_ref[...] = k
    v_ref[...] = v.astype(BF)
    for t in range(3):
        new_ref[128 * t:128 * t + 128] = k[:, 128 * t:128 * t + 128]
    new_ref[384:768] = v.T.astype(BF)


def attn_body(sets, has_new, has_prev, *refs):
    len_ref, *refs = refs
    metas, refs = refs[:4], refs[4:]
    q_refs, refs = refs[:8], refs[8:]
    kv_refs, refs = refs[:len(sets)], refs[len(sets):]
    new_refs, refs = (refs[:2], refs[2:]) if has_new else ((), refs)
    prev_refs, refs = (refs[:8], refs[8:]) if has_prev else ((), refs)
    out_refs, refs = refs[:8], refs[8:]
    kv, qa, oa, qm, s_ref, acc, idx, cnt, val, sem = refs
    nc = HALF * len(sets)
    z = lax.axis_index("z")
    core = lax.axis_index("c")
    req0 = 2 * lax.axis_index("yl")
    nreq = lax.div(z, 4)
    npos = [(lax.rem(z, 4) * 2 + core) * 128, (lax.rem(z, 4) * 2 + 1 - core) * 128]
    for i, ref in enumerate(new_refs):
        pltpu.make_async_copy(ref, kv.at[nc + i], sem.at[nc + i]).start()
    for r in range(2):
        cnt[r] = 0
        idx[r, 0] = 0
    uses = []
    for i, (m, first) in enumerate(sets):
        for b in range(HALF):
            j = HALF * i + b
            o = metas[m][0, first + b] - req0
            use = (o >= 0) & (o < 2)
            uses.append(use)

            @pl.when(use)
            def _():
                pltpu.make_async_copy(kv_refs[i].at[b], kv.at[j], sem.at[j]).start()
                val[j] = jnp.clip(len_ref[o + req0] - metas[m][1, first + b], 0, 128)
                c = cnt[o]
                idx[o, c] = j
                cnt[o] = c + 1

    for d in range(8):
        qa[lax.rem(z + d, 8)] = q_refs[d][...]
        if has_prev:
            oa[lax.rem(z + d, 8)] = prev_refs[d][...]
    for i, ref in enumerate(new_refs):
        pltpu.make_async_copy(ref, kv.at[nc + i], sem.at[nc + i]).wait()
    for i, (m, first) in enumerate(sets):
        for b in range(HALF):
            j = HALF * i + b

            @pl.when(uses[j])
            def _():
                pltpu.make_async_copy(kv_refs[i].at[b], kv.at[j], sem.at[j]).wait()

    ii = lax.broadcasted_iota(I32, (128, 256), 0)
    lane = lax.broadcasted_iota(I32, (1, 256), 1)
    hrow = lax.broadcasted_iota(I32, (384, 256), 0)

    def pair(pr, carry):
        r = lax.div(pr, 2)
        start = lax.rem(pr, 2) * 512 + core * 128
        tp = start + jnp.where(lane < 128, lane, lane + 128)
        q = jnp.concatenate([qa[2 * pr], qa[2 * pr + 1]], axis=1)
        for h in range(4):
            for w, t in enumerate(WIN[h]):
                rr = hrow[128 * t:128 * t + 128]
                sel = (rr >= HD * h) & (rr < HD * h + HD)
                block = q[128 * t:128 * t + 128].astype(F32)
                qm[h, 128 * w:128 * w + 128] = jnp.where(sel, block, 0.0).astype(BF)
        cached = cnt[r]
        for i in range(len(new_refs)):
            @pl.when((nreq == r) & (npos[i] <= start + 256))
            def _():
                c = cnt[r]
                idx[r, c] = nc + i
                cnt[r] = c + 1
        n = cnt[r]
        cnt[r] = cached
        idx[r, n] = idx[r, 0]
        steps = lax.div(n + 1, 2)

        def entry(k):
            j = idx[r, k]
            live = k < n
            isn = live & (j >= nc)
            np_ = jnp.where(j == nc, npos[0], npos[1])
            v = jnp.where(live & (j < nc), val[jnp.minimum(j, nc - 1)], 0)
            full = jnp.where(isn, start - np_ >= 127, v >= 128)
            return j, isn, np_, v, full

        def scores(g, m):
            e = [entry(2 * g), entry(2 * g + 1)]
            mm = []
            for h in range(4):
                rows = [
                    jnp.concatenate([kv[x[0], 128 * t:128 * t + 128] for t in WIN[h]], axis=1)
                    for x in e
                ]
                lhs = jnp.concatenate(rows, axis=0)
                s = jnp.dot(lhs, qm[h, 0:128 * len(WIN[h])], preferred_element_type=F32)
                s_ref[g, h] = s
                mm.append(jnp.maximum(m[h], jnp.max(s.reshape(32, 8, 256), axis=0)))

            def masked():
                out = []
                for h in range(4):
                    top = m[h]
                    for x in range(2):
                        _, isn, np_, v, _ = e[x]
                        thr = jnp.where(isn, tp - np_, v - 1)
                        s = jnp.where(ii <= thr, s_ref[g, h, 128 * x:128 * x + 128], NEG)
                        s_ref[g, h, 128 * x:128 * x + 128] = s
                        top = jnp.maximum(top, jnp.max(s.reshape(16, 8, 256), axis=0))
                    out.append(top)
                return tuple(out)

            return lax.cond(e[0][4] & e[1][4], lambda: tuple(mm), masked)

        m = lax.fori_loop(0, steps, scores, tuple(jnp.full((8, 256), NEG, F32) for _ in range(4)))
        mx = [jnp.maximum(jnp.max(m[h], axis=0, keepdims=True), FLOOR) for h in range(4)]
        acc[...] = jnp.zeros_like(acc)

        def weigh(g, l):
            j0 = idx[r, 2 * g]
            j1 = idx[r, 2 * g + 1]
            nl = []
            for h in range(4):
                w = jnp.exp(s_ref[g, h] - mx[h])
                nl.append(l[h] + jnp.sum(w.reshape(32, 8, 256), axis=0))
                at = slice(384 + HD * h, 384 + HD * h + HD)
                vt = jnp.concatenate([kv[j0, at], kv[j1, at]], axis=1)
                acc[h] += jnp.dot(vt, w.astype(BF), preferred_element_type=F32)
            return tuple(nl)

        l = lax.fori_loop(0, steps, weigh, tuple(jnp.zeros((8, 256), F32) for _ in range(4)))
        terms = [[], [], []]
        if has_prev:
            old = jnp.concatenate([oa[2 * pr, 384:400], oa[2 * pr + 1, 384:400]], axis=1).astype(F32)
            old = old[0:4] + old[4:8] + old[8:12]
        for h in range(4):
            at = slice(HD * h, HD * h + HD)
            total = jnp.sum(l[h], axis=0, keepdims=True)
            has = total > 0
            safe = jnp.where(has, total, 1.0)
            lse = jnp.where(has, mx[h] + jnp.log(safe), NEG)
            inv = 1.0 / safe
            if has_prev:
                top = jnp.maximum(lse, old[h:h + 1])
                w_new = jnp.exp(lse - top)
                w_old = jnp.exp(old[h:h + 1] - top)
                both = w_new + w_old
                lse = top + jnp.log(both)
                before = jnp.concatenate([oa[2 * pr, at], oa[2 * pr + 1, at]], axis=1).astype(F32)
                o = acc[h] * (inv * w_new / both) + before * (w_old / both)
            else:
                o = acc[h] * inv
            o = o.astype(BF)
            oa[2 * pr, at] = o[:, :128]
            oa[2 * pr + 1, at] = o[:, 128:]
            for term in terms:
                part = lse.astype(BF).astype(F32)
                term.append(part)
                lse = lse - part
        rows = terms[0] + terms[1] + terms[2] + [jnp.zeros((4, 256), F32)]
        st = jnp.concatenate(rows, axis=0).astype(BF)
        oa[2 * pr, 384:400] = st[:, :128]
        oa[2 * pr + 1, 384:400] = st[:, 128:]
        return carry

    lax.fori_loop(0, 4, pair, 0)
    for d in range(8):
        out_refs[d][...] = oa[lax.rem(z + d, 8)]


def attn(sets, lens, metas, qs, kvs, news=(), prev=()):
    nb = HALF * len(sets) + 2
    return pl.pallas_call(
        functools.partial(attn_body, sets, bool(news), bool(prev)),
        in_specs=[SM] * 5 + [VM] * 8 + [HBM] * (len(kvs) + len(news)) + [VM] * len(prev),
        out_specs=[VM] * 8,
        out_shape=[S((400, 128), BF)] * 8,
        scratch_shapes=[
            pltpu.VMEM((nb, 768, 128), BF),
            pltpu.VMEM((8, 384, 128), BF),
            pltpu.VMEM((8, 400, 128), BF),
            pltpu.VMEM((4, 256, 256), BF),
            pltpu.VMEM((nb // 2, 4, 256, 256), F32),
            pltpu.VMEM((4, HD, 256), F32),
            pltpu.SMEM((2, nb + 1), I32),
            pltpu.SMEM((2,), I32),
            pltpu.SMEM((nb,), I32),
            pltpu.SemaphoreType.DMA((nb,)),
        ],
        name="attn",
    )(lens, *metas, *qs, *kvs, *news, *prev)


def combine_body(*refs):
    o_ref = refs[-1]
    parts = refs[:-1]
    lses = []
    for p in parts:
        st = p[384:400].astype(F32)
        lses.append(st[0:4] + st[4:8] + st[8:12])
    top = functools.reduce(jnp.maximum, lses)
    ws = [jnp.exp(x - top) for x in lses]
    inv = 1.0 / functools.reduce(jnp.add, ws)
    ws = [w * inv for w in ws]
    rows = []
    for h in range(4):
        acc = jnp.zeros((HD, 128), F32)
        for p, w in zip(parts, ws):
            acc = acc + p[HD * h:HD * h + HD].astype(F32) * w[h:h + 1]
        rows.append(acc)
    o_ref[...] = jnp.concatenate(rows, axis=0).T.astype(BF)


def layer(features, gain, w_qkv, rope_factors, cache_len, cache_kv, block_owner, block_base):
    swap = ring(2, 1)

    f1 = lax.ppermute(features, "yh", swap)
    kv0a = prep(cache_kv, 0)
    kv2a = lax.ppermute(kv0a, "yl", swap)
    both = jnp.concatenate([features, f1], axis=0)
    fm = lax.ppermute(both, "x", ring(4, 2))
    fr = lax.ppermute(both, "x", ring(4, 1))
    fl = lax.ppermute(both, "x", ring(4, -1))

    kv0b = prep(cache_kv, HALF)
    kv2b = lax.ppermute(kv0b, "yl", swap)
    kv1a = lax.ppermute(kv0a, "c", swap)
    kv1b = lax.ppermute(kv0b, "c", swap)
    kv3a = lax.ppermute(kv2a, "c", swap)
    kv3b = lax.ppermute(kv2b, "c", swap)
    meta = jnp.stack([block_owner, block_base])
    m2 = lax.ppermute(meta, "yl", swap)
    m1 = lax.ppermute(meta, "c", swap)
    m3 = lax.ppermute(m2, "c", swap)
    metas = [meta, m1, m2, m3]

    z = lax.axis_index("z")
    request = 2 * lax.axis_index("yl") + z // 4
    start = ((z % 4) * 2 + lax.axis_index("c")) * 128
    positions = cache_len[request] + start + jnp.arange(128, dtype=I32)
    inv_freq = 1.0 / (rope_factors * jnp.power(10000.0, jnp.arange(48, dtype=F32) * 2.0 / HD))
    angles = inv_freq[:, None] * positions.astype(F32)[None, :]
    cos = jnp.cos(angles) * MSCALE
    sin = jnp.sin(angles) * MSCALE

    w = w_qkv.transpose(1, 0, 2)
    q, normed = pl.pallas_call(
        query_body,
        in_specs=[VM] * 8 + [HBM],
        out_specs=[VM, VM],
        out_shape=[S((384, 128), BF), S((8, 128, 384), BF)],
        scratch_shapes=[pltpu.VMEM((8, 384, 384), BF), pltpu.SemaphoreType.DMA((8,))],
        name="query",
    )(gain.reshape(8, 1, 384), cos, sin, features, f1, fr, fl, fm, w)
    qs = [q] + [None] * 7
    for d in DIST:
        qs[d] = lax.ppermute(q, "z", ring(8, -d))
    new0, kn, vn = pl.pallas_call(
        keyval_body,
        in_specs=[VM] * 3 + [HBM],
        out_specs=[VM, VM, VM],
        out_shape=[S((768, 128), BF), S((128, 384), BF), S((128, 384), BF)],
        scratch_shapes=[pltpu.VMEM((2, 8, 384, 384), BF), pltpu.SemaphoreType.DMA((2, 8))],
        name="keyval",
    )(cos, sin, normed, w)
    new_kv = jnp.stack([kn, vn], axis=1)
    new1 = lax.ppermute(new0, "c", swap)
    sets = ((0, 0), (0, HALF), (1, 0), (1, HALF), (2, 0), (3, 0))
    parts = attn(sets, cache_len, metas, qs, [kv0a, kv0b, kv1a, kv1b, kv2a, kv3a], [new0, new1])
    sets = ((2, HALF), (3, HALF))
    parts = attn(sets, cache_len, metas, qs, [kv2b, kv3b], prev=parts)
    got = [parts[0]]
    for d in DIST:
        got.append(lax.ppermute(parts[d], "z", ring(8, d)))
    attended = pl.pallas_call(
        combine_body,
        in_specs=[VM] * 8,
        out_specs=VM,
        out_shape=S((128, 384), BF),
        name="combine",
    )(*got)
    return attended, new_kv


def solution(mesh):
    wide = Mesh(mesh.devices.reshape(2, 8, 2, 2, 4), ("yl", "z", "c", "yh", "x"))
    seq = ("yl", "z", "c")
    ten = ("yh", "x")
    in_specs = (
        P(seq, ten),
        P(),
        P(None, None, ten),
        P(),
        P(),
        P(seq, None, None, ten),
        P(seq),
        P(seq),
    )
    out_specs = (P(seq, ten), P(seq, None, ten))
    return jax.shard_map(layer, mesh=wide, in_specs=in_specs, out_specs=out_specs, check_vma=False)
```

```python
import functools

import jax
import jax.numpy as jnp
from jax import lax
from jax.experimental import pallas as pl
from jax.experimental.pallas import tpu as pltpu
from jax.sharding import Mesh, PartitionSpec as P


S = jax.ShapeDtypeStruct
EPSILON = 1e-05
NEG = -1e30
FLOOR = -1e29
MSCALE = 1.1902380714238083
F32 = jnp.float32
BF = jnp.bfloat16
I32 = jnp.int32
VM = pl.BlockSpec(memory_space=pltpu.VMEM)
SM = pl.BlockSpec(memory_space=pltpu.SMEM)
HBM = pl.BlockSpec(memory_space=pl.ANY)
HD = 96
HALF = 6
WIN = ((0,), (0, 1), (1, 2), (2,))


def ring(n, k):
    return [(i, (i + k) % n) for i in range(n)]


def pick(first):
    i = lax.broadcasted_iota(I32, (128, 256), 0)
    j = lax.broadcasted_iota(I32, (128, 256), 1)
    return (j == 2 * i + first).astype(F32).astype(BF)


def prep_body(kv_ref, o_ref):
    x = kv_ref[...].reshape(256, 384)
    k = jnp.dot(pick(0), x, preferred_element_type=F32).astype(BF)
    v = jnp.dot(pick(1), x, preferred_element_type=F32)
    for t in range(3):
        o_ref[128 * t:128 * t + 128] = k[:, 128 * t:128 * t + 128]
    o_ref[384:768] = v.T.astype(BF)


def prep(kv, first):
    return pl.pallas_call(
        prep_body,
        grid=(HALF,),
        in_specs=[pl.BlockSpec((None, 128, 2, 384), lambda i: (i + first, 0, 0, 0))],
        out_specs=pl.BlockSpec((None, 768, 128), lambda i: (i, 0, 0)),
        out_shape=S((HALF, 768, 128), BF),
        name="prep",
    )(kv)


def rotate(t, cos, sin):
    out = []
    for h in range(4):
        a = t[HD * h:HD * h + 48]
        b = t[HD * h + 48:HD * h + 96]
        out.append(a * cos - b * sin)
        out.append(b * cos + a * sin)
    return jnp.concatenate(out, axis=0)


def chunk_ids():
    yh = lax.axis_index("yh")
    x = lax.axis_index("x")
    ids = []
    for dx in (0, 3, 1, 2):
        xs = lax.rem(x + dx, 4)
        ids += [yh * 4 + xs, (1 - yh) * 4 + xs]
    return ids


def query_body(gain_ref, cos_ref, sin_ref, f0, f1, fr, fl, fm, w_hbm, q_ref, n_ref, wbuf, sem):
    ids = chunk_ids()
    copies = []
    for j in range(8):
        rows = pl.ds(pl.multiple_of(ids[j] * 384, 384), 384)
        c = pltpu.make_async_copy(w_hbm.at[0, rows], wbuf.at[j], sem.at[j])
        c.start()
        copies.append(c)
    chunks = [f0[...], f1[...]]
    for f in (fr, fl, fm):
        chunks += [f[0:128], f[128:256]]
    wide = [c.astype(F32) for c in chunks]
    total = jnp.zeros((128, 384), F32)
    for x in wide:
        total = total + x * x
    scale = lax.rsqrt(jnp.sum(total, axis=1, keepdims=True) * (1.0 / 3072) + EPSILON)
    acc = jnp.zeros((128, 384), F32)
    for j in range(8):
        n = (wide[j] * scale * gain_ref[ids[j]]).astype(BF)
        n_ref[j] = n
        copies[j].wait()
        acc = acc + jnp.dot(n, wbuf[j], preferred_element_type=F32)
    q_ref[...] = (rotate(acc.T, cos_ref[...], sin_ref[...]) * HD ** (-0.5)).astype(BF)


def keyval_body(cos_ref, sin_ref, n_ref, w_hbm, new_ref, k_ref, v_ref, wbuf, sem):
    ids = chunk_ids()
    copies = []
    for c in range(2):
        for j in range(8):
            rows = pl.ds(pl.multiple_of(ids[j] * 384, 384), 384)
            d = pltpu.make_async_copy(w_hbm.at[1 + c, rows], wbuf.at[c, j], sem.at[c, j])
            d.start()
            copies.append(d)
    accs = []
    for c in range(2):
        acc = jnp.zeros((128, 384), F32)
        for j in range(8):
            copies[8 * c + j].wait()
            acc = acc + jnp.dot(n_ref[j], wbuf[c, j], preferred_element_type=F32)
        accs.append(acc)
    k = rotate(accs[0].T, cos_ref[...], sin_ref[...]).T.astype(BF)
    v = accs[1]
    k_ref[...] = k
    v_ref[...] = v.astype(BF)
    for t in range(3):
        new_ref[128 * t:128 * t + 128] = k[:, 128 * t:128 * t + 128]
    new_ref[384:768] = v.T.astype(BF)


def attn_body(sets, has_new, has_prev, *refs):
    len_ref, *refs = refs
    metas, refs = refs[:4], refs[4:]
    q_refs, refs = refs[:8], refs[8:]
    kv_refs, refs = refs[:len(sets)], refs[len(sets):]
    new_refs, refs = (refs[:2], refs[2:]) if has_new else ((), refs)
    prev_refs, refs = (refs[:8], refs[8:]) if has_prev else ((), refs)
    out_refs, refs = refs[:8], refs[8:]
    kv, qa, oa, qm, s_ref, acc, idx, cnt, val, sem = refs
    nc = HALF * len(sets)
    z = lax.axis_index("z")
    core = lax.axis_index("c")
    req0 = 2 * lax.axis_index("yl")
    nreq = lax.div(z, 4)
    npos = [(lax.rem(z, 4) * 2 + core) * 128, (lax.rem(z, 4) * 2 + 1 - core) * 128]
    for i, ref in enumerate(new_refs):
        pltpu.make_async_copy(ref, kv.at[nc + i], sem.at[nc + i]).start()
    for r in range(2):
        cnt[r] = 0
        idx[r, 0] = 0
    uses = []
    for i, (m, first) in enumerate(sets):
        for b in range(HALF):
            j = HALF * i + b
            o = metas[m][0, first + b] - req0
            use = (o >= 0) & (o < 2)
            uses.append(use)

            @pl.when(use)
            def _():
                pltpu.make_async_copy(kv_refs[i].at[b], kv.at[j], sem.at[j]).start()
                val[j] = jnp.clip(len_ref[o + req0] - metas[m][1, first + b], 0, 128)
                c = cnt[o]
                idx[o, c] = j
                cnt[o] = c + 1

    for d in range(8):
        qa[lax.rem(z + d, 8)] = q_refs[d][...]
        if has_prev:
            oa[lax.rem(z + d, 8)] = prev_refs[d][...]
    for i, ref in enumerate(new_refs):
        pltpu.make_async_copy(ref, kv.at[nc + i], sem.at[nc + i]).wait()
    for i, (m, first) in enumerate(sets):
        for b in range(HALF):
            j = HALF * i + b

            @pl.when(uses[j])
            def _():
                pltpu.make_async_copy(kv_refs[i].at[b], kv.at[j], sem.at[j]).wait()

    ii = lax.broadcasted_iota(I32, (128, 256), 0)
    lane = lax.broadcasted_iota(I32, (1, 256), 1)
    hrow = lax.broadcasted_iota(I32, (384, 256), 0)

    def pair(pr, carry):
        r = lax.div(pr, 2)
        start = lax.rem(pr, 2) * 512 + core * 128
        tp = start + jnp.where(lane < 128, lane, lane + 128)
        q = jnp.concatenate([qa[2 * pr], qa[2 * pr + 1]], axis=1)
        for h in range(4):
            for w, t in enumerate(WIN[h]):
                rr = hrow[128 * t:128 * t + 128]
                sel = (rr >= HD * h) & (rr < HD * h + HD)
                block = q[128 * t:128 * t + 128]
                qm[h, 128 * w:128 * w + 128] = jnp.where(sel, block, jnp.zeros_like(block))
        cached = cnt[r]
        for i in range(len(new_refs)):
            @pl.when((nreq == r) & (npos[i] <= start + 256))
            def _():
                c = cnt[r]
                idx[r, c] = nc + i
                cnt[r] = c + 1
        n = cnt[r]
        cnt[r] = cached
        idx[r, n] = idx[r, 0]
        steps = lax.div(n + 1, 2)

        def entry(k):
            j = idx[r, k]
            live = k < n
            isn = live & (j >= nc)
            np_ = jnp.where(j == nc, npos[0], npos[1])
            v = jnp.where(live & (j < nc), val[jnp.minimum(j, nc - 1)], 0)
            full = jnp.where(isn, start - np_ >= 127, v >= 128)
            return j, isn, np_, v, full

        def scores(g, m):
            e = [entry(2 * g), entry(2 * g + 1)]
            mm = []
            for h in range(4):
                rows = [
                    jnp.concatenate([kv[x[0], 128 * t:128 * t + 128] for t in WIN[h]], axis=1)
                    for x in e
                ]
                lhs = jnp.concatenate(rows, axis=0)
                s = jnp.dot(lhs, qm[h, 0:128 * len(WIN[h])], preferred_element_type=F32)
                s_ref[g, h] = s
                mm.append(jnp.maximum(m[h], jnp.max(s.reshape(32, 8, 256), axis=0)))

            def masked():
                out = []
                for h in range(4):
                    top = m[h]
                    for x in range(2):
                        _, isn, np_, v, _ = e[x]
                        thr = jnp.where(isn, tp - np_, v - 1)
                        s = jnp.where(ii <= thr, s_ref[g, h, 128 * x:128 * x + 128], NEG)
                        s_ref[g, h, 128 * x:128 * x + 128] = s
                        top = jnp.maximum(top, jnp.max(s.reshape(16, 8, 256), axis=0))
                    out.append(top)
                return tuple(out)

            return lax.cond(e[0][4] & e[1][4], lambda: tuple(mm), masked)

        m = lax.fori_loop(0, steps, scores, tuple(jnp.full((8, 256), NEG, F32) for _ in range(4)))
        mx = [jnp.maximum(jnp.max(m[h], axis=0, keepdims=True), FLOOR) for h in range(4)]
        acc[...] = jnp.zeros_like(acc)

        def weigh(g, l):
            j0 = idx[r, 2 * g]
            j1 = idx[r, 2 * g + 1]
            nl = []
            for h in range(4):
                w = jnp.exp(s_ref[g, h] - mx[h])
                nl.append(l[h] + jnp.sum(w.reshape(32, 8, 256), axis=0))
                at = slice(384 + HD * h, 384 + HD * h + HD)
                vt = jnp.concatenate([kv[j0, at], kv[j1, at]], axis=1)
                acc[h] += jnp.dot(vt, w.astype(BF), preferred_element_type=F32)
            return tuple(nl)

        l = lax.fori_loop(0, steps, weigh, tuple(jnp.zeros((8, 256), F32) for _ in range(4)))
        terms = [[], [], []]
        if has_prev:
            old = jnp.concatenate([oa[2 * pr, 384:400], oa[2 * pr + 1, 384:400]], axis=1).astype(F32)
            old = old[0:4] + old[4:8] + old[8:12]
        for h in range(4):
            at = slice(HD * h, HD * h + HD)
            total = jnp.sum(l[h], axis=0, keepdims=True)
            has = total > 0
            safe = jnp.where(has, total, 1.0)
            lse = jnp.where(has, mx[h] + jnp.log(safe), NEG)
            inv = 1.0 / safe
            if has_prev:
                top = jnp.maximum(lse, old[h:h + 1])
                w_new = jnp.exp(lse - top)
                w_old = jnp.exp(old[h:h + 1] - top)
                both = w_new + w_old
                lse = top + jnp.log(both)
                before = jnp.concatenate([oa[2 * pr, at], oa[2 * pr + 1, at]], axis=1).astype(F32)
                o = acc[h] * (inv * w_new / both) + before * (w_old / both)
            else:
                o = acc[h] * inv
            o = o.astype(BF)
            oa[2 * pr, at] = o[:, :128]
            oa[2 * pr + 1, at] = o[:, 128:]
            for term, part in zip(terms, thirds(lse)):
                term.append(part)
        rows = terms[0] + terms[1] + terms[2] + [jnp.zeros((4, 256), F32)]
        st = jnp.concatenate(rows, axis=0).astype(BF)
        oa[2 * pr, 384:400] = st[:, :128]
        oa[2 * pr + 1, 384:400] = st[:, 128:]
        return carry

    lax.fori_loop(0, 4, pair, 0)
    for d in range(8):
        out_refs[d][...] = oa[lax.rem(z + d, 8)]


def attn(sets, lens, metas, qs, kvs, news=(), prev=()):
    nb = HALF * len(sets) + 2
    return pl.pallas_call(
        functools.partial(attn_body, sets, bool(news), bool(prev)),
        in_specs=[SM] * 5 + [VM] * 8 + [HBM] * (len(kvs) + len(news)) + [VM] * len(prev),
        out_specs=[VM] * 8,
        out_shape=[S((400, 128), BF)] * 8,
        scratch_shapes=[
            pltpu.VMEM((nb, 768, 128), BF),
            pltpu.VMEM((8, 384, 128), BF),
            pltpu.VMEM((8, 400, 128), BF),
            pltpu.VMEM((4, 256, 256), BF),
            pltpu.VMEM((nb // 2, 4, 256, 256), F32),
            pltpu.VMEM((4, HD, 256), F32),
            pltpu.SMEM((2, nb + 1), I32),
            pltpu.SMEM((2,), I32),
            pltpu.SMEM((nb,), I32),
            pltpu.SemaphoreType.DMA((nb,)),
        ],
        name="attn",
    )(lens, *metas, *qs, *kvs, *news, *prev)


def merged(parts):
    lses = []
    for p in parts:
        st = p[384:400].astype(F32)
        lses.append(st[0:4] + st[4:8] + st[8:12])
    top = functools.reduce(jnp.maximum, lses)
    ws = [jnp.exp(x - top) for x in lses]
    total = functools.reduce(jnp.add, ws)
    inv = 1.0 / total
    ws = [w * inv for w in ws]
    rows = []
    for h in range(4):
        acc = jnp.zeros((HD, 128), F32)
        for p, w in zip(parts, ws):
            acc = acc + p[HD * h:HD * h + HD].astype(F32) * w[h:h + 1]
        rows.append(acc)
    return jnp.concatenate(rows, axis=0), top + jnp.log(total)


def thirds(lse):
    out = []
    for _ in range(3):
        part = lse.astype(BF).astype(F32)
        out.append(part)
        lse = lse - part
    return out


def merge_body(p2, r3, p6, r5, r4, m2, m6):
    for parts, o_ref in (((p2, r3), m2), ((p6, r5, r4), m6)):
        o, lse = merged(parts)
        o_ref[0:384] = o.astype(BF)
        o_ref[384:400] = jnp.concatenate(thirds(lse) + [jnp.zeros((4, 128), F32)], axis=0).astype(BF)


def combine_body(*refs):
    o, _ = merged(refs[:-1])
    refs[-1][...] = o.T.astype(BF)


def layer(features, gain, w_qkv, rope_factors, cache_len, cache_kv, block_owner, block_base):
    swap = ring(2, 1)

    f1 = lax.ppermute(features, "yh", swap)
    kv0a = prep(cache_kv, 0)
    kv2a = lax.ppermute(kv0a, "yl", swap)
    both = jnp.concatenate([features, f1], axis=0)
    fm = lax.ppermute(both, "x", ring(4, 2))
    fr = lax.ppermute(both, "x", ring(4, 1))
    fl = lax.ppermute(both, "x", ring(4, -1))

    kv0b = prep(cache_kv, HALF)
    kv2b = lax.ppermute(kv0b, "yl", swap)
    kv1a = lax.ppermute(kv0a, "c", swap)
    kv1b = lax.ppermute(kv0b, "c", swap)
    kv3a = lax.ppermute(kv2a, "c", swap)
    kv3b = lax.ppermute(kv2b, "c", swap)
    meta = jnp.stack([block_owner, block_base])
    m2 = lax.ppermute(meta, "yl", swap)
    m1 = lax.ppermute(meta, "c", swap)
    m3 = lax.ppermute(m2, "c", swap)
    metas = [meta, m1, m2, m3]

    z = lax.axis_index("z")
    request = 2 * lax.axis_index("yl") + z // 4
    start = ((z % 4) * 2 + lax.axis_index("c")) * 128
    length = jnp.sum(jnp.where(jnp.arange(4) == request, cache_len, 0))
    positions = length + start + jnp.arange(128, dtype=I32)
    inv_freq = 1.0 / (rope_factors * jnp.power(10000.0, jnp.arange(48, dtype=F32) * 2.0 / HD))
    angles = inv_freq[:, None] * positions.astype(F32)[None, :]
    cos = jnp.cos(angles) * MSCALE
    sin = jnp.sin(angles) * MSCALE

    w = w_qkv.transpose(1, 0, 2)
    q, normed = pl.pallas_call(
        query_body,
        in_specs=[VM] * 8 + [HBM],
        out_specs=[VM, VM],
        out_shape=[S((384, 128), BF), S((8, 128, 384), BF)],
        scratch_shapes=[pltpu.VMEM((8, 384, 384), BF), pltpu.SemaphoreType.DMA((8,))],
        name="query",
    )(gain.reshape(8, 1, 384), cos, sin, features, f1, fr, fl, fm, w)
    qs = [q] + [None] * 7
    for d in (2, 6, 1, 7):
        qs[d] = lax.ppermute(q, "z", ring(8, -d))
    for d, source, hop in ((4, 6, 2), (3, 2, -1), (5, 6, 1)):
        qs[d] = lax.ppermute(qs[source], "z", ring(8, hop))
    new0, kn, vn = pl.pallas_call(
        keyval_body,
        in_specs=[VM] * 3 + [HBM],
        out_specs=[VM, VM, VM],
        out_shape=[S((768, 128), BF), S((128, 384), BF), S((128, 384), BF)],
        scratch_shapes=[pltpu.VMEM((2, 8, 384, 384), BF), pltpu.SemaphoreType.DMA((2, 8))],
        name="keyval",
    )(cos, sin, normed, w)
    new_kv = jnp.stack([kn, vn], axis=1)
    new1 = lax.ppermute(new0, "c", swap)
    sets = ((0, 0), (0, HALF), (1, 0), (1, HALF), (2, 0), (3, 0))
    parts = attn(sets, cache_len, metas, qs, [kv0a, kv0b, kv1a, kv1b, kv2a, kv3a], [new0, new1])
    sets = ((2, HALF), (3, HALF))
    parts = attn(sets, cache_len, metas, qs, [kv2b, kv3b], prev=parts)
    r4 = lax.ppermute(parts[4], "z", ring(8, -2))
    r3 = lax.ppermute(parts[3], "z", ring(8, 1))
    r5 = lax.ppermute(parts[5], "z", ring(8, -1))
    g1 = lax.ppermute(parts[1], "z", ring(8, 1))
    g7 = lax.ppermute(parts[7], "z", ring(8, -1))
    m2, m6 = pl.pallas_call(
        merge_body,
        in_specs=[VM] * 5,
        out_specs=[VM] * 2,
        out_shape=[S((400, 128), BF)] * 2,
        name="merge",
    )(parts[2], r3, parts[6], r5, r4)
    g2 = lax.ppermute(m2, "z", ring(8, 2))
    g6 = lax.ppermute(m6, "z", ring(8, -2))
    attended = pl.pallas_call(
        combine_body,
        in_specs=[VM] * 5,
        out_specs=VM,
        out_shape=S((128, 384), BF),
        name="combine",
    )(parts[0], g1, g7, g2, g6)
    return attended, new_kv


def solution(mesh):
    wide = Mesh(mesh.devices.reshape(2, 8, 2, 2, 4), ("yl", "z", "c", "yh", "x"))
    seq = ("yl", "z", "c")
    ten = ("yh", "x")
    in_specs = (
        P(seq, ten),
        P(),
        P(None, None, ten),
        P(),
        P(),
        P(seq, None, None, ten),
        P(seq),
        P(seq),
    )
    out_specs = (P(seq, ten), P(seq, None, ten))
    return jax.shard_map(layer, mesh=wide, in_specs=in_specs, out_specs=out_specs, check_vma=False)
```
